256 devices in a mesh: expert: 32 (over x, z), src: 8 (over y, core).
Axes of the slice: x: 4, y: 4, z: 8, core: 2. Of those that a mesh axis runs over, the one named last changes fastest.
Arguments:
- tokens: bfloat16 [32768, 4096], P(('expert', 'src')), may hold values from -6 to 6
- expert_id: int32 [32768, 1], P(('expert', 'src')), may hold values from 0 to 31; in each aligned block of 128 rows (0 to 127, 128 to 255, ...) at most 5 rows name the same one
- gate: float32 [32768], P(('expert', 'src')), may hold values from 0.2 to 1
- w_in: bfloat16 [32, 4096, 5120], P('expert', None, 'src'), may hold values from -0.09375 to 0.09375
- w_out: bfloat16 [32, 5120, 4096], P('expert', 'src'), may hold values from -0.078125 to 0.078125
- keys: bfloat16 [12288, 4096], P(('expert', 'src')), may hold values from -6 to 6
- values: bfloat16 [12288, 4096], P(('expert', 'src')), may hold values from -6 to 6
- query_gain: float32 [4096], replicated, may hold values from 0.1 to 1.9
Outputs:
- result: bfloat16 [32768, 4096], P(('expert', 'src'))
The draws below stay inside these ranges and needn't reach their ends.
Inputs may be any that keep to these rules, and one draw needn't show every extreme that they name: `expert_id`: in each block of 128 rows (the rows of one device) no expert is named by more than 5 rows, a bound that some block reaches.
All inputs are finite; a program needn't handle non-finite values.
Results may differ from the reference program's by a relative error of at most 0.01.
Values may be sent and summed in bfloat16 or wider, within the bound.
No kernel may reach another device: no remote copies, remote signals or barrier semaphores. Data moves between devices by JAX's collectives and lax.ppermute only.
A program may use at most 128 MiB of HBM per device.

```python
import math
import jax
import jax.numpy as jnp
import numpy as np
from jax import lax

D = 4096
FF = 5120
HEAD_DIM = 64
HEADS = 64
EXPERTS = 32
TOK_DEV = 128
CAP = 5
TGT_LEN = 1024
SRC_LEN = 384
TOKENS = 32768
SOURCES = 12288
N_SRC = 8


def draw_tokens(key, part):
    base_key = jax.random.fold_in(key, 4211)
    base_draw = jnp.clip(jax.random.normal(base_key, (TOKENS, D), jnp.float32), -6.0, 6.0)
    return base_draw.astype(jnp.bfloat16)


def draw_keys(key, part):
    base_key = jax.random.fold_in(key, 5527)
    base_draw = jnp.clip(jax.random.normal(base_key, (SOURCES, D), jnp.float32), -6.0, 6.0)
    return base_draw.astype(jnp.bfloat16)


def level_of(key, extent, cuts, smallest, largest):
    def one(dim, shards_of):
        steps = jax.random.uniform(jax.random.fold_in(jax.random.fold_in(key, 6), dim), (shards_of,), jnp.float32, smallest / len(cuts), largest / len(cuts))
        return jnp.repeat(jnp.exp(steps), extent[dim] // shards_of).reshape((-1,) + (1,) * (len(extent) - dim - 1))

    factor_of = one(*cuts[0])
    for cut in cuts[1:]:
        factor_of = factor_of * one(*cut)
    return factor_of


def routed_block(stream_key, own, number, rows, number_of, top, most, skew):
    ranking = jax.random.permutation(stream_key, number_of)
    heavy_load, usual = load_shares(number_of, rows * top, most, skew, True), load_shares(number_of, rows * top, most, skew, False)
    places = jnp.arange(number_of)

    def named(sizes, rotation):
        used = int((sizes > 0).sum())
        fixed = max(1, used // 4)
        moved = fixed + (places - fixed + rotation * (used - fixed)) % max(1, number_of - fixed)
        return jnp.zeros((number_of,), jnp.int32).at[ranking[jnp.where(places < fixed, places, moved)]].set(jnp.asarray(sizes, jnp.int32))

    sizes = jnp.where(number % 4 == 0, named(heavy_load, number // 4), named(usual, number - number // 4 - 1))
    mixed = jax.random.permutation(jax.random.fold_in(own, 3), number_of)
    donor, receiver = mixed[0:number_of // 2 * 2:2], mixed[1:number_of // 2 * 2:2]
    room = jnp.minimum(sizes[donor] - 1, most - sizes[receiver]) // 2
    room = jnp.where((donor == ranking[0]) | (receiver == ranking[0]) | (sizes[receiver] == 0), 0, jnp.maximum(room, 0))
    moved = jax.random.randint(jax.random.fold_in(own, 4), (number_of // 2,), 0, 1 << 20) % (room + 1)
    sizes = sizes.at[donor].add(-moved).at[receiver].add(moved)
    labels = jnp.searchsorted(jnp.cumsum(sizes), jnp.arange(rows * top), side="right").astype(jnp.int32)
    grid = labels.reshape(top, rows).T
    grid = grid[jax.random.permutation(jax.random.fold_in(own, 1), rows)]
    rotation = jax.random.randint(jax.random.fold_in(own, 2), (rows, 1), 0, top)
    return jnp.take_along_axis(grid, (jnp.arange(top)[None, :] + rotation) % top, axis=1)


def load_shares(number_of, total, reach, lean, full):
    portions = [(1 << 20) // math.isqrt(grade ** lean) + 1 for grade in range(1, number_of + 1)]
    largest = reach if full else min(reach, max(-(-total // number_of), total * portions[0] // sum(portions)))
    least = 1 if total - largest >= number_of - 1 else 0
    given, surplus = [largest] + [least] * (number_of - 1), total - largest - least * (number_of - 1)
    while surplus > 0:
        free = [i for i in range(1, number_of) if given[i] < largest] or [i for i in range(1, number_of) if given[i] < reach]
        mass, remaining = sum([portions[i] for i in free]), surplus
        for i in free:
            addition = min(reach - given[i], max(1, remaining * portions[i] // mass), surplus)
            given[i] = given[i] + addition
            surplus = surplus - addition
    return np.array(given)


def scatter_about(key, extent, width, limit, shards=(), held_as=jnp.bfloat16):
    values = width * jax.random.normal(key, extent, jnp.float32)
    if shards:
        values = values * level_of(key, extent, shards, -0.22, 0.18)
    return jnp.clip(values, -limit, limit).astype(held_as)


def setup_inputs(seed: int = 0) -> dict:
    streams_of = jax.random.split(jax.random.key(seed), 9)
    tokens = draw_tokens(jax.random.fold_in(streams_of[8], 71), 0)
    expert_id_keys = jax.random.split(jax.random.fold_in(streams_of[1], 1), TOKENS // TOK_DEV)
    expert_id_turns = jax.random.permutation(jax.random.fold_in(streams_of[1], 3), TOKENS // TOK_DEV)
    expert_id = jax.vmap(lambda own, number: routed_block(jax.random.fold_in(streams_of[1], 2), own, number, TOK_DEV, EXPERTS, 1, CAP, 2))(expert_id_keys, expert_id_turns).reshape((TOKENS, 1))
    gate = jnp.clip(0.2 + 0.8 * jax.random.uniform(streams_of[2], (TOKENS,), jnp.float32) ** level_of(streams_of[2], (TOKENS,), ((0, 256),), -0.2, 0.2), 0.2, 1.0)
    w_in = scatter_about(streams_of[3], (EXPERTS, D, FF), D ** -0.5, 0.09375, ((0, 32), (2, 8)))
    w_out = scatter_about(streams_of[4], (EXPERTS, FF, D), FF ** -0.5, 0.078125, ((0, 32), (1, 8)))
    keys = draw_keys(jax.random.fold_in(streams_of[8], 71), 0)
    values = scatter_about(streams_of[6], (SOURCES, D), 1.0, 6.0, ((0, 256),))
    query_gain = jnp.clip(1.0 + 0.18 * jax.random.normal(streams_of[7], (D,), jnp.float32), 0.1, 1.9)
    return {"tokens": tokens, "expert_id": expert_id, "gate": gate, "w_in": w_in, "w_out": w_out, "keys": keys, "values": values, "query_gain": query_gain}


def expert_pass(packed):
    expert_rows, w_first, w_second = packed
    hidden = jax.nn.relu(jnp.dot(expert_rows, w_first, preferred_element_type=jnp.float32)).astype(jnp.bfloat16)
    hidden = lax.optimization_barrier(hidden).astype(jnp.float32)
    hidden = hidden.reshape(hidden.shape[0], N_SRC, FF // N_SRC)
    second_wide = w_second.astype(jnp.float32).reshape(N_SRC, FF // N_SRC, D)
    partial_value = jnp.einsum('rjf,jfd->jrd', hidden, second_wide).astype(jnp.bfloat16)
    partial_value = lax.optimization_barrier(partial_value).astype(jnp.float32)
    return lax.optimization_barrier(jnp.sum(partial_value, axis=0)).astype(jnp.bfloat16)

def attend(packed):
    query_rows, key_rows, value_rows = packed
    query_heads = query_rows.astype(jnp.float32).reshape(TGT_LEN, HEADS, HEAD_DIM)
    key_heads = key_rows.astype(jnp.float32).reshape(SRC_LEN, HEADS, HEAD_DIM)
    value_heads = value_rows.astype(jnp.float32).reshape(SRC_LEN, HEADS, HEAD_DIM)
    scores = jnp.einsum('thd,shd->hts', query_heads, key_heads) * HEAD_DIM ** (-0.5)
    row_peak = lax.optimization_barrier(jnp.max(scores, axis=2, keepdims=True))
    raw_weights = jnp.exp(scores - row_peak)
    weight_sum = lax.optimization_barrier(jnp.sum(raw_weights, axis=2))
    rounded = lax.optimization_barrier(raw_weights.astype(jnp.bfloat16)).astype(jnp.float32)
    mixed_sum = jnp.einsum('hts,shd->thd', rounded, value_heads)
    context = mixed_sum / jnp.transpose(weight_sum)[:, :, None]
    return context.reshape(TGT_LEN, D)

def reference(tokens, expert_id, gate, w_in, w_out, keys, values, query_gain):
    block_count = TOKENS // TOK_DEV
    token_expert = expert_id[:, 0].reshape(block_count, TOK_DEV)
    one_hot = (token_expert[:, :, None] == jnp.arange(EXPERTS, dtype=jnp.int32)[None, None, :]).astype(jnp.int32)
    earlier = jnp.cumsum(one_hot, axis=1) - one_hot
    slot = lax.optimization_barrier(jnp.sum(earlier * one_hot, axis=2)).astype(jnp.int32)
    position = (token_expert * CAP + slot).astype(jnp.int32)
    block_index = jnp.arange(block_count, dtype=jnp.int32)[:, None]
    token_blocks = tokens.reshape(block_count, TOK_DEV, D)
    buffer = jnp.zeros((block_count, EXPERTS * CAP, D), jnp.bfloat16)
    buffer = buffer.at[block_index, position].set(token_blocks)
    buffer = buffer.reshape(block_count, EXPERTS, CAP, D).transpose(1, 0, 2, 3).reshape(EXPERTS, block_count * CAP, D)
    expert_out = lax.map(expert_pass, (buffer, w_in, w_out))
    answers = expert_out.reshape(EXPERTS, block_count, CAP, D).transpose(1, 0, 2, 3).reshape(block_count, EXPERTS * CAP, D)
    picked = answers[block_index, position].astype(jnp.float32).reshape(TOKENS, D)
    mixed = (tokens.astype(jnp.float32) + gate[:, None] * picked).astype(jnp.bfloat16)
    mixed_wide = mixed.astype(jnp.float32)
    inv_norm = lax.rsqrt(lax.optimization_barrier(jnp.mean(mixed_wide * mixed_wide, axis=1, keepdims=True)) + 1e-06)
    query_rows = (mixed_wide * inv_norm * query_gain[None, :]).astype(jnp.bfloat16)
    sequences = TOKENS // TGT_LEN
    context = lax.map(attend, (query_rows.reshape(sequences, TGT_LEN, D), keys.reshape(sequences, SRC_LEN, D), values.reshape(sequences, SRC_LEN, D)))
    return (mixed_wide + context.reshape(TOKENS, D)).astype(jnp.bfloat16)
```

```python
import functools

import jax
import jax.numpy as jnp
from jax import lax
from jax.experimental import pallas as pl
from jax.experimental.pallas import tpu as pltpu
from jax.sharding import PartitionSpec as P

HEAD_DIM = 64
CORES = 2
SLOT_CHUNKS = (2, 3)
LANES = 128


def along_y(step):
    devices = lax.axis_size("src")
    rows = devices // CORES
    return [
        (y * CORES + c, ((y + step) % rows) * CORES + c) for y in range(rows) for c in range(CORES)
    ]


def shift(array, step):
    return lax.ppermute(array, "src", along_y(step))


def swap_cores(array):
    return lax.ppermute(array, "src", [(s, s ^ 1) for s in range(lax.axis_size("src"))])


def ffn_kernel(first_steps, *refs):
    blocks = refs[:4]
    first_own, first_other, second_own, second_other = refs[4:8]
    outs = refs[8:12]
    hidden_own, hidden_other = refs[12:14]
    step = pl.program_id(0)

    @pl.when(step < first_steps)
    def _():
        rows = jnp.concatenate([b[...] for b in blocks], axis=0)
        weight = jnp.concatenate([first_own[...], first_other[...]], axis=1)
        hidden = jnp.dot(rows, weight, preferred_element_type=jnp.float32)
        hidden = jnp.maximum(hidden, 0.0).astype(jnp.bfloat16)
        half = weight.shape[1] // 2
        hidden_own[step] = hidden[:, :half]
        hidden_other[step] = hidden[:, half:]

    @pl.when(step >= first_steps)
    def _():
        hidden = jnp.concatenate(
            [hidden_own[j] for j in range(first_steps)]
            + [hidden_other[j] for j in range(first_steps)],
            axis=1,
        )
        weight = jnp.concatenate([second_own[...], second_other[...]], axis=0)
        partial = jnp.dot(hidden, weight, preferred_element_type=jnp.float32).astype(jnp.bfloat16)
        size = outs[0].shape[0]
        for n, out in enumerate(outs):
            out[...] = partial[n * size : (n + 1) * size]


def ffn(blocks, first_own, first_other, second_own, second_other):
    size, width = blocks[0].shape
    hidden = first_own.shape[1]
    first_tile, second_tile = 128, 512
    first_steps, second_steps = hidden // first_tile, width // second_tile
    block_spec = pl.BlockSpec((size, width), lambda i: (0, 0))
    first_spec = pl.BlockSpec((width, first_tile), lambda i: (0, jnp.minimum(i, first_steps - 1)))
    second_spec = pl.BlockSpec((hidden, second_tile), lambda i: (0, jnp.maximum(i - first_steps, 0)))
    out_spec = pl.BlockSpec((size, second_tile), lambda i: (0, jnp.maximum(i - first_steps, 0)))
    total = 4 * size
    return pl.pallas_call(
        functools.partial(ffn_kernel, first_steps),
        grid=(first_steps + second_steps,),
        in_specs=[block_spec] * 4 + [first_spec] * 2 + [second_spec] * 2,
        out_specs=[out_spec] * 4,
        out_shape=[jax.ShapeDtypeStruct((size, width), jnp.bfloat16)] * 4,
        scratch_shapes=[
            pltpu.VMEM((first_steps, total, first_tile), jnp.bfloat16),
            pltpu.VMEM((first_steps, total, first_tile), jnp.bfloat16),
        ],
        cost_estimate=pl.CostEstimate(
            flops=8 * total * width * hidden,
            bytes_accessed=8 * width * hidden + 4 * total * width,
            transcendentals=0,
        ),
        compiler_params=pltpu.CompilerParams(vmem_limit_bytes=48 << 20),
        name="ffn",
    )(*blocks, first_own, first_other, second_own, second_other)


def add(*parts):
    total = parts[0].astype(jnp.float32)
    for part in parts[1:]:
        total = total + part.astype(jnp.float32)
    return total.astype(jnp.bfloat16)


def exchange(rows):
    experts = lax.axis_size("expert")
    count, width = rows.shape
    blocks = rows.reshape(experts, count * width // (experts * LANES), LANES)
    blocks = lax.all_to_all(blocks, "expert", split_axis=0, concat_axis=0, tiled=True)
    return blocks.reshape(count, width)


def per_device(tokens, expert_id, gate, w_in, w_out, keys, values, query_gain):
    tok_rows, model_width = tokens.shape
    expert_count = lax.axis_size("expert")
    token_expert = expert_id[:, 0]
    one_hot = (
        token_expert[:, None] == lax.broadcasted_iota(jnp.int32, (tok_rows, expert_count), 1)
    ).astype(jnp.bfloat16)
    before = (
        lax.broadcasted_iota(jnp.int32, (tok_rows, tok_rows), 0)
        > lax.broadcasted_iota(jnp.int32, (tok_rows, tok_rows), 1)
    ).astype(jnp.bfloat16)
    earlier = jnp.dot(before, one_hot, preferred_element_type=jnp.float32)
    slot = jnp.sum(earlier * one_hot.astype(jnp.float32), axis=1).astype(jnp.int32)

    all_keys = lax.all_gather(keys, "src", axis=0, tiled=True)
    all_values = lax.all_gather(values, "src", axis=0, tiled=True)

    first_own, second_own = w_in[0], w_out[0]
    first_other, second_other = swap_cores(first_own), swap_cores(second_own)

    placings = []
    first_slot = 0
    for count in SLOT_CHUNKS:
        local = slot - first_slot
        spot = jnp.where((local >= 0) & (local < count), token_expert * count + local, -1)
        placings.append(
            (
                spot[:, None]
                == lax.broadcasted_iota(jnp.int32, (tok_rows, expert_count * count), 1)
            ).astype(jnp.bfloat16)
        )
        first_slot += count

    arrived = []
    for placing in placings:
        outgoing = jnp.einsum(
            "rk,rd->kd", placing, tokens, preferred_element_type=jnp.float32
        ).astype(jnp.bfloat16)
        arrived.append(exchange(outgoing))

    picked = None
    for n, (placing, own) in enumerate(zip(placings, arrived)):
        way = 1 if n % 2 == 0 else -1
        near = shift(own, way)
        back = shift(own, -way)
        far = shift(near, way)
        p_own, p_near, p_back, p_far = ffn(
            (own, near, back, far), first_own, first_other, second_own, second_other
        )
        passing = shift(p_far, -way)
        from_back = shift(p_back, way)
        joined = shift(add(p_near, passing), -way)
        summed = add(p_own, from_back, joined)
        returned = exchange(summed)
        part = jnp.dot(placing, returned, preferred_element_type=jnp.float32)
        picked = part if picked is None else picked + part

    mixed_wide = (
        (tokens.astype(jnp.float32) + gate[:, None] * picked)
        .astype(jnp.bfloat16)
        .astype(jnp.float32)
    )
    inv_norm = lax.rsqrt(jnp.mean(mixed_wide * mixed_wide, axis=1, keepdims=True) + 1e-06)
    query_rows = (mixed_wide * inv_norm * query_gain[None, :]).astype(jnp.bfloat16)
    head_count = model_width // HEAD_DIM
    query_heads = query_rows.reshape(tok_rows, head_count, HEAD_DIM)
    score_scale = HEAD_DIM ** (-0.5)
    key_heads = all_keys.reshape(all_keys.shape[0], head_count, HEAD_DIM)
    scores = (
        jnp.einsum("thd,shd->hts", query_heads, key_heads, preferred_element_type=jnp.float32)
        * score_scale
    )
    row_peak = jnp.max(scores, axis=2, keepdims=True)
    raw_weights = jnp.exp(scores - row_peak)
    weight_sum = jnp.sum(raw_weights, axis=2)
    value_heads = all_values.reshape(all_values.shape[0], head_count, HEAD_DIM)
    mixed_sum = jnp.einsum(
        "hts,shd->thd",
        raw_weights.astype(jnp.bfloat16),
        value_heads,
        preferred_element_type=jnp.float32,
    )
    context = mixed_sum / jnp.transpose(weight_sum)[:, :, None]
    return (mixed_wide + context.reshape(tok_rows, model_width)).astype(jnp.bfloat16)


def solution(mesh):
    return jax.shard_map(
        per_device,
        mesh=mesh,
        in_specs=(
            P(("expert", "src"), None),
            P(("expert", "src"), None),
            P(("expert", "src")),
            P("expert", None, "src"),
            P("expert", "src", None),
            P(("expert", "src"), None),
            P(("expert", "src"), None),
            P(),
        ),
        out_specs=P(("expert", "src"), None),
        check_vma=False,
    )
```

```python
import functools

import jax
import jax.numpy as jnp
from jax import lax
from jax.experimental import pallas as pl
from jax.experimental.pallas import tpu as pltpu
from jax.sharding import PartitionSpec as P


HEAD_DIM = 64
CORES = 2
SLOT_CHUNKS = (3, 2)
LANES = 128


def along_y(step):
    devices = lax.axis_size("src")
    rows = devices // CORES
    return [
        (y * CORES + c, ((y + step) % rows) * CORES + c) for y in range(rows) for c in range(CORES)
    ]


def shift(array, step):
    return lax.ppermute(array, "src", along_y(step))


def in_hbm(array):
    return pltpu.with_memory_space_constraint(array, pltpu.HBM)


def swap_cores(array):
    return lax.ppermute(array, "src", [(s, s ^ 1) for s in range(lax.axis_size("src"))])


def prepare_kernel(ids, gate, tokens, meta, *refs):
    outs, stage = refs[:-1], refs[-1]
    tok_rows, width = tokens.shape
    experts = outs[0].shape[0]
    chosen = ids[...]
    one_hot = (
        chosen == lax.broadcasted_iota(jnp.int32, (experts, tok_rows), 0)
    ).astype(jnp.float32)
    before = (
        lax.broadcasted_iota(jnp.int32, (tok_rows, tok_rows), 0)
        < lax.broadcasted_iota(jnp.int32, (tok_rows, tok_rows), 1)
    ).astype(jnp.bfloat16)
    earlier = jnp.dot(one_hot.astype(jnp.bfloat16), before, preferred_element_type=jnp.float32)
    slot = jnp.sum(earlier * one_hot, axis=0, keepdims=True).astype(jnp.int32)
    meta[...] = jnp.zeros_like(meta)
    meta[0:1] = gate[...]
    first_slot = 0
    groups = width // LANES
    tile = 512
    for n, (count, out) in enumerate(zip(SLOT_CHUNKS, outs)):
        local = slot - first_slot
        spot = jnp.where((local >= 0) & (local < count), chosen * count + local, -1)
        meta[n + 1 : n + 2] = spot.astype(jnp.float32)
        rows = experts * count
        placing = (spot == lax.broadcasted_iota(jnp.int32, (rows, tok_rows), 0)).astype(
            jnp.bfloat16
        )
        for start in range(0, width, tile):
            value = jnp.dot(
                placing, tokens[:, start : start + tile], preferred_element_type=jnp.float32
            )
            for part in range(tile // LANES):
                stage[pl.ds(start // LANES + part, rows, stride=groups), :] = value[
                    :, part * LANES : (part + 1) * LANES
                ]
        out[...] = (
            stage[: rows * groups].astype(jnp.bfloat16).reshape(experts, count * groups, LANES)
        )
        first_slot += count


def prepare(ids, gate, tokens):
    tok_rows, width = tokens.shape
    experts = lax.axis_size("expert")
    groups = width // LANES
    near = pl.BlockSpec(memory_space=pltpu.VMEM)
    return pl.pallas_call(
        prepare_kernel,
        in_specs=[near] * 3,
        out_specs=[near] * (1 + len(SLOT_CHUNKS)),
        out_shape=[jax.ShapeDtypeStruct((8, tok_rows), jnp.float32)]
        + [
            jax.ShapeDtypeStruct((experts, count * groups, LANES), jnp.bfloat16)
            for count in SLOT_CHUNKS
        ],
        scratch_shapes=[pltpu.VMEM((experts * max(SLOT_CHUNKS) * groups, LANES), jnp.float32)],
        compiler_params=pltpu.CompilerParams(vmem_limit_bytes=8 << 20),
        name="prepare",
    )(in_hbm(ids), in_hbm(gate), in_hbm(tokens))


def first_kernel(*refs):
    blocks, firsts, out = refs[:-6], refs[-6:-4], refs[-4]
    rows, pieces, sems = refs[-3:]
    units = firsts[0].shape[1]
    count, tile = pieces.shape[0], pieces.shape[2] // CORES

    def copy(piece, owner):
        return pltpu.make_async_copy(
            firsts[owner].at[:, pl.ds(pl.multiple_of(piece * tile, tile), tile)],
            pieces.at[piece, :, pl.ds(owner * tile, tile)],
            sems.at[piece, owner],
        )

    for piece in range(count):
        for owner in range(CORES):
            copy(piece, owner).start()
    row = 0
    for block in blocks:
        rows[row : row + block.shape[0]] = block[...]
        row += block.shape[0]

    def body(piece, carry):
        for owner in range(CORES):
            copy(piece, owner).wait()
        value = jnp.dot(rows[...], pieces[piece], preferred_element_type=jnp.float32)
        value = jnp.maximum(value, 0.0).astype(jnp.bfloat16)
        for owner in range(CORES):
            start = pl.multiple_of(owner * units + piece * tile, tile)
            out[:, pl.ds(start, tile)] = value[:, owner * tile : (owner + 1) * tile]
        return carry

    lax.fori_loop(0, count, body, 0)


def second_kernel(*refs):
    hidden, seconds, outs = refs[0], refs[1:3], refs[3:-2]
    pieces, sems = refs[-2:]
    units = seconds[0].shape[0]
    count, tile = pieces.shape[0], pieces.shape[2]

    def copy(piece, owner):
        return pltpu.make_async_copy(
            seconds[owner].at[:, pl.ds(pl.multiple_of(piece * tile, tile), tile)],
            pieces.at[piece, pl.ds(owner * units, units), :],
            sems.at[piece, owner],
        )

    for piece in range(count):
        for owner in range(CORES):
            copy(piece, owner).start()

    def body(piece, carry):
        for owner in range(CORES):
            copy(piece, owner).wait()
        value = jnp.dot(hidden[...], pieces[piece], preferred_element_type=jnp.float32)
        value = value.astype(jnp.bfloat16)
        start = pl.multiple_of(piece * tile, tile)
        row = 0
        for out in outs:
            out[:, pl.ds(start, tile)] = value[row : row + out.shape[0]]
            row += out.shape[0]
        return carry

    lax.fori_loop(0, count, body, 0)


def first_layer(blocks, firsts):
    width, units = firsts[0].shape
    total = sum(block.shape[0] for block in blocks)
    tile = 128
    count = units // tile
    near = pl.BlockSpec(memory_space=pltpu.VMEM)
    return pl.pallas_call(
        first_kernel,
        in_specs=[near] * len(blocks) + [pl.BlockSpec(memory_space=pltpu.HBM)] * CORES,
        out_specs=near,
        out_shape=jax.ShapeDtypeStruct((total, CORES * units), jnp.bfloat16),
        scratch_shapes=[
            pltpu.VMEM((total, width), jnp.bfloat16),
            pltpu.VMEM((count, width, CORES * tile), jnp.bfloat16),
            pltpu.SemaphoreType.DMA((count, CORES)),
        ],
        cost_estimate=pl.CostEstimate(
            flops=4 * total * width * units,
            bytes_accessed=4 * width * units + 2 * total * width,
            transcendentals=0,
        ),
        compiler_params=pltpu.CompilerParams(vmem_limit_bytes=20 << 20),
        name="first",
    )(*blocks, *firsts)


def second_layer(hidden, seconds, sizes):
    units, width = seconds[0].shape
    total = hidden.shape[0]
    tile = 1024
    count = width // tile
    near = pl.BlockSpec(memory_space=pltpu.VMEM)
    return pl.pallas_call(
        second_kernel,
        in_specs=[near] + [pl.BlockSpec(memory_space=pltpu.HBM)] * CORES,
        out_specs=[near] * len(sizes),
        out_shape=[jax.ShapeDtypeStruct((size, width), jnp.bfloat16) for size in sizes],
        scratch_shapes=[
            pltpu.VMEM((count, CORES * units, tile), jnp.bfloat16),
            pltpu.SemaphoreType.DMA((count, CORES)),
        ],
        cost_estimate=pl.CostEstimate(
            flops=4 * total * width * units,
            bytes_accessed=4 * width * units + 2 * total * width,
            transcendentals=0,
        ),
        compiler_params=pltpu.CompilerParams(vmem_limit_bytes=16 << 20),
        name="second",
    )(hidden, *seconds)


def finish_kernel(chunks, *refs):
    tokens, meta, gain = refs[:3]
    returned, sources = refs[3 : 3 + chunks], refs[3 + chunks : -3]
    out, mixed, query = refs[-3:]
    keys, values = sources[:8], sources[8:]
    step = pl.program_id(0)
    groups, tok_rows, tile = mixed.shape
    score_scale = HEAD_DIM ** (-0.5)

    @pl.when(step == 0)
    def _():
        placings = [
            (
                meta[n + 1 : n + 2].astype(jnp.int32)
                == lax.broadcasted_iota(jnp.int32, (rows.shape[0], tok_rows), 0)
            ).astype(jnp.bfloat16)
            for n, rows in enumerate(returned)
        ]
        diagonal = lax.broadcasted_iota(
            jnp.int32, (tok_rows, tok_rows), 0
        ) == lax.broadcasted_iota(jnp.int32, (tok_rows, tok_rows), 1)
        gate = jnp.sum(jnp.where(diagonal, meta[0:1], 0.0), axis=1, keepdims=True)
        square = jnp.zeros((tok_rows, 1), jnp.float32)
        for g in range(groups):
            lanes = slice(g * tile, (g + 1) * tile)
            picked = sum(
                lax.dot_general(
                    placing,
                    rows[:, lanes],
                    (((0,), (0,)), ((), ())),
                    preferred_element_type=jnp.float32,
                )
                for placing, rows in zip(placings, returned)
            )
            value = tokens[:, lanes].astype(jnp.float32) + gate * picked
            value = value.astype(jnp.bfloat16)
            mixed[g] = value
            wide = value.astype(jnp.float32)
            square = square + jnp.sum(wide * wide, axis=1, keepdims=True)
        inv_norm = lax.rsqrt(square * (1.0 / (groups * tile)) + 1e-06)
        for g in range(groups):
            lanes = slice(g * tile, (g + 1) * tile)
            value = (mixed[g].astype(jnp.float32) * inv_norm * gain[:, lanes]).astype(jnp.bfloat16)
            query[g] = value * jnp.bfloat16(score_scale)

    low = lax.broadcasted_iota(jnp.int32, (tok_rows, LANES), 1) < HEAD_DIM
    zero = jnp.zeros((tok_rows, LANES), jnp.bfloat16)
    for pair in range(tile // LANES):
        lanes = slice(pair * LANES, (pair + 1) * LANES)
        q = query[step, :, lanes]
        k = jnp.concatenate([ref[:, lanes] for ref in keys], axis=0)
        v = jnp.concatenate([ref[:, lanes] for ref in values], axis=0)
        heads = []
        for head, masked in enumerate((jnp.where(low, q, zero), jnp.where(low, zero, q))):
            scores = lax.dot_general(
                k, masked, (((1,), (1,)), ((), ())), preferred_element_type=jnp.float32
            )
            raw = jnp.exp(scores - jnp.max(scores, axis=0, keepdims=True))
            weight_sum = jnp.sum(raw, axis=0, keepdims=True)
            both = lax.dot_general(
                v,
                raw.astype(jnp.bfloat16),
                (((0,), (0,)), ((), ())),
                preferred_element_type=jnp.float32,
            )
            both = both * (1.0 / weight_sum)
            heads.append(both[head * HEAD_DIM : (head + 1) * HEAD_DIM])
        context = jnp.concatenate(heads, axis=0).T
        out[:, lanes] = (mixed[step, :, lanes].astype(jnp.float32) + context).astype(jnp.bfloat16)


def finish(tokens, meta, gain, returned, sources):
    tok_rows, width = tokens.shape
    tile = 1024
    groups = width // tile
    source_rows = sum(piece.shape[0] for piece in sources) // 2

    def whole(array):
        return pl.BlockSpec(array.shape, lambda i: (0, 0))

    def part(array):
        return pl.BlockSpec((array.shape[0], tile), lambda i: (0, i))

    fixed = [in_hbm(tokens), in_hbm(meta), in_hbm(gain), *returned]
    return pl.pallas_call(
        functools.partial(finish_kernel, len(returned)),
        grid=(groups,),
        in_specs=[whole(a) for a in fixed] + [part(a) for a in sources],
        out_specs=pl.BlockSpec((tok_rows, tile), lambda i: (0, i)),
        out_shape=jax.ShapeDtypeStruct((tok_rows, width), jnp.bfloat16),
        scratch_shapes=[
            pltpu.VMEM((groups, tok_rows, tile), jnp.bfloat16),
            pltpu.VMEM((groups, tok_rows, tile), jnp.bfloat16),
        ],
        cost_estimate=pl.CostEstimate(
            flops=8 * tok_rows * source_rows * width,
            bytes_accessed=4 * source_rows * width + 8 * tok_rows * width,
            transcendentals=tok_rows * source_rows * width // HEAD_DIM,
        ),
        compiler_params=pltpu.CompilerParams(vmem_limit_bytes=20 << 20),
        name="finish",
    )(*fixed, *sources)


def add(one, other):
    return (one.astype(jnp.float32) + other.astype(jnp.float32)).astype(jnp.bfloat16)


def merge_kernel(*refs):
    parts, out, stage = refs[:6], refs[6], refs[7]
    rows, width = parts[0].shape
    groups = width // LANES
    tile = 512
    for side in range(2):
        for start in range(0, width, tile):
            value = sum(
                part[:, start : start + tile].astype(jnp.float32)
                for part in parts[3 * side : 3 * side + 3]
            )
            for lane in range(0, tile, LANES):
                first = side * rows * groups + (start + lane) // LANES
                stage[pl.ds(first, rows, stride=groups), :] = value[:, lane : lane + LANES]
    out[...] = stage[...].astype(jnp.bfloat16).reshape(out.shape)


def merge(parts, experts):
    rows, width = parts[0].shape
    groups = width // LANES
    near = pl.BlockSpec(memory_space=pltpu.VMEM)
    return pl.pallas_call(
        merge_kernel,
        in_specs=[near] * 6,
        out_specs=near,
        out_shape=jax.ShapeDtypeStruct((experts, 2 * rows * groups // experts, LANES), jnp.bfloat16),
        scratch_shapes=[pltpu.VMEM((2 * rows * groups, LANES), jnp.float32)],
        cost_estimate=pl.CostEstimate(
            flops=6 * rows * width, bytes_accessed=16 * rows * width, transcendentals=0
        ),
        compiler_params=pltpu.CompilerParams(vmem_limit_bytes=8 << 20),
        name="merge",
    )(*parts)


def exchange(blocks):
    return lax.all_to_all(blocks, "expert", split_axis=0, concat_axis=0, tiled=True)


def per_device(tokens, expert_id, gate, w_in, w_out, keys, values, query_gain):
    tok_rows, model_width = tokens.shape
    meta, *outgoing = prepare(expert_id.reshape(1, tok_rows), gate[None, :], tokens)

    firsts, seconds = [
        [in_hbm(w) for w in (own, swap_cores(own))]
        for own in (w_in[0], w_out[0])
    ]

    near = [shift(piece, 1) for piece in (keys, values)]
    back = [shift(piece, -1) for piece in (keys, values)]
    far_keys = shift(near[0], 1)
    far_values = shift(back[1], -1)
    sources = []
    for piece in (keys, near[0], back[0], far_keys, values, near[1], back[1], far_values):
        sources.extend((piece, swap_cores(piece)))

    returned = []
    arrived = [exchange(blocks) for blocks in outgoing]
    for blocks in arrived:
        experts = blocks.shape[0]
        a, b = [
            half.reshape(-1, model_width)
            for half in (blocks[: experts // 2], blocks[experts // 2 :])
        ]
        near_a = shift(a, 1)
        back_b = shift(b, -1)
        near_b = shift(b, 1)
        back_a = shift(a, -1)
        low = shift(near_a, 1)
        high = shift(back_b, -1)
        halves = (a, b, near_a, near_b, back_a, back_b, low, high)
        hidden = first_layer(halves, firsts)
        halves = second_layer(hidden, seconds, [half.shape[0] for half in halves])
        a, b, near_a, near_b, back_a, back_b, low, high = halves
        low = shift(low, -1)
        high = shift(high, 1)
        near_b = shift(near_b, -1)
        back_a = shift(back_a, 1)
        near_a = shift(add(near_a, low), -1)
        back_b = shift(add(back_b, high), 1)
        summed = merge((a, near_a, back_a, b, near_b, back_b), experts)
        returned.append(exchange(summed).reshape(-1, model_width))

    return finish(
        tokens,
        meta,
        query_gain[None, :],
        returned,
        sources,
    )


def solution(mesh):
    return jax.shard_map(
        per_device,
        mesh=mesh,
        in_specs=(
            P(("expert", "src"), None),
            P(("expert", "src"), None),
            P(("expert", "src")),
            P("expert", None, "src"),
            P("expert", "src", None),
            P(("expert", "src"), None),
            P(("expert", "src"), None),
            P(),
        ),
        out_specs=P(("expert", "src"), None),
        check_vma=False,
    )
```

```python
import functools

import jax
import jax.numpy as jnp
from jax import lax
from jax.experimental import pallas as pl
from jax.experimental.pallas import tpu as pltpu
from jax.sharding import PartitionSpec as P


HEAD_DIM = 64
CORES = 2
SLOT_CHUNKS = (3, 2)
LANES = 128


def along_y(step):
    devices = lax.axis_size("src")
    rows = devices // CORES
    return [
        (y * CORES + c, ((y + step) % rows) * CORES + c) for y in range(rows) for c in range(CORES)
    ]


def shift(array, step):
    return lax.ppermute(array, "src", along_y(step))


def in_hbm(array):
    return pltpu.with_memory_space_constraint(array, pltpu.HBM)


def swap_cores(array):
    return lax.ppermute(array, "src", [(s, s ^ 1) for s in range(lax.axis_size("src"))])


def prepare_kernel(ids, gate, tokens, meta, *refs):
    outs, stage = refs[:-1], refs[-1]
    tok_rows, width = tokens.shape
    experts = outs[0].shape[0]
    chosen = ids[...]
    one_hot = (
        chosen == lax.broadcasted_iota(jnp.int32, (experts, tok_rows), 0)
    ).astype(jnp.float32)
    before = (
        lax.broadcasted_iota(jnp.int32, (tok_rows, tok_rows), 0)
        < lax.broadcasted_iota(jnp.int32, (tok_rows, tok_rows), 1)
    ).astype(jnp.bfloat16)
    earlier = jnp.dot(one_hot.astype(jnp.bfloat16), before, preferred_element_type=jnp.float32)
    slot = jnp.sum(earlier * one_hot, axis=0, keepdims=True).astype(jnp.int32)
    meta[...] = jnp.zeros_like(meta)
    meta[0:1] = gate[...]
    first_slot = 0
    groups = width // LANES
    tile = 512
    for n, (count, out) in enumerate(zip(SLOT_CHUNKS, outs)):
        local = slot - first_slot
        spot = jnp.where((local >= 0) & (local < count), chosen * count + local, -1)
        meta[n + 1 : n + 2] = spot.astype(jnp.float32)
        rows = experts * count
        placing = (spot == lax.broadcasted_iota(jnp.int32, (rows, tok_rows), 0)).astype(
            jnp.bfloat16
        )
        for start in range(0, width, tile):
            value = jnp.dot(
                placing, tokens[:, start : start + tile], preferred_element_type=jnp.float32
            )
            for part in range(tile // LANES):
                stage[pl.ds(start // LANES + part, rows, stride=groups), :] = value[
                    :, part * LANES : (part + 1) * LANES
                ]
        out[...] = (
            stage[: rows * groups].astype(jnp.bfloat16).reshape(experts, count * groups, LANES)
        )
        first_slot += count


def prepare(ids, gate, tokens):
    tok_rows, width = tokens.shape
    experts = lax.axis_size("expert")
    groups = width // LANES
    near = pl.BlockSpec(memory_space=pltpu.VMEM)
    return pl.pallas_call(
        prepare_kernel,
        in_specs=[near] * 3,
        out_specs=[near] * (1 + len(SLOT_CHUNKS)),
        out_shape=[jax.ShapeDtypeStruct((8, tok_rows), jnp.float32)]
        + [
            jax.ShapeDtypeStruct((experts, count * groups, LANES), jnp.bfloat16)
            for count in SLOT_CHUNKS
        ],
        scratch_shapes=[pltpu.VMEM((experts * max(SLOT_CHUNKS) * groups, LANES), jnp.float32)],
        compiler_params=pltpu.CompilerParams(vmem_limit_bytes=8 << 20),
        name="prepare",
    )(in_hbm(ids), in_hbm(gate), in_hbm(tokens))


def first_kernel(*refs):
    blocks, firsts, out = refs[:-6], refs[-6:-4], refs[-4]
    rows, pieces, sems = refs[-3:]
    units = firsts[0].shape[1]
    count, tile = pieces.shape[0], pieces.shape[2] // CORES

    def copy(piece, owner):
        return pltpu.make_async_copy(
            firsts[owner].at[:, pl.ds(pl.multiple_of(piece * tile, tile), tile)],
            pieces.at[piece, :, pl.ds(owner * tile, tile)],
            sems.at[piece, owner],
        )

    for piece in range(count):
        for owner in range(CORES):
            copy(piece, owner).start()
    row = 0
    for block in blocks:
        rows[row : row + block.shape[0]] = block[...]
        row += block.shape[0]

    def body(piece, carry):
        for owner in range(CORES):
            copy(piece, owner).wait()
        value = jnp.dot(rows[...], pieces[piece], preferred_element_type=jnp.float32)
        value = jnp.maximum(value, 0.0).astype(jnp.bfloat16)
        for owner in range(CORES):
            start = pl.multiple_of(owner * units + piece * tile, tile)
            out[:, pl.ds(start, tile)] = value[:, owner * tile : (owner + 1) * tile]
        return carry

    lax.fori_loop(0, count, body, 0)


def second_kernel(*refs):
    hidden, seconds, outs = refs[0], refs[1:3], refs[3:-2]
    pieces, sems = refs[-2:]
    units = seconds[0].shape[0]
    count, tile = pieces.shape[0], pieces.shape[2]

    def copy(piece, owner):
        return pltpu.make_async_copy(
            seconds[owner].at[:, pl.ds(pl.multiple_of(piece * tile, tile), tile)],
            pieces.at[piece, pl.ds(owner * units, units), :],
            sems.at[piece, owner],
        )

    for piece in range(count):
        for owner in range(CORES):
            copy(piece, owner).start()

    def body(piece, carry):
        for owner in range(CORES):
            copy(piece, owner).wait()
        value = jnp.dot(hidden[...], pieces[piece], preferred_element_type=jnp.float32)
        value = value.astype(jnp.bfloat16)
        start = pl.multiple_of(piece * tile, tile)
        row = 0
        for out in outs:
            out[:, pl.ds(start, tile)] = value[row : row + out.shape[0]]
            row += out.shape[0]
        return carry

    lax.fori_loop(0, count, body, 0)


def first_layer(blocks, firsts):
    width, units = firsts[0].shape
    total = sum(block.shape[0] for block in blocks)
    tile = 128
    count = units // tile
    near = pl.BlockSpec(memory_space=pltpu.VMEM)
    return pl.pallas_call(
        first_kernel,
        in_specs=[near] * len(blocks) + [pl.BlockSpec(memory_space=pltpu.HBM)] * CORES,
        out_specs=near,
        out_shape=jax.ShapeDtypeStruct((total, CORES * units), jnp.bfloat16),
        scratch_shapes=[
            pltpu.VMEM((total, width), jnp.bfloat16),
            pltpu.VMEM((count, width, CORES * tile), jnp.bfloat16),
            pltpu.SemaphoreType.DMA((count, CORES)),
        ],
        cost_estimate=pl.CostEstimate(
            flops=4 * total * width * units,
            bytes_accessed=4 * width * units + 2 * total * width,
            transcendentals=0,
        ),
        compiler_params=pltpu.CompilerParams(vmem_limit_bytes=20 << 20),
        name="first",
    )(*blocks, *firsts)


def second_layer(hidden, seconds, sizes):
    units, width = seconds[0].shape
    total = hidden.shape[0]
    tile = 1024
    count = width // tile
    near = pl.BlockSpec(memory_space=pltpu.VMEM)
    return pl.pallas_call(
        second_kernel,
        in_specs=[near] + [pl.BlockSpec(memory_space=pltpu.HBM)] * CORES,
        out_specs=[near] * len(sizes),
        out_shape=[jax.ShapeDtypeStruct((size, width), jnp.bfloat16) for size in sizes],
        scratch_shapes=[
            pltpu.VMEM((count, CORES * units, tile), jnp.bfloat16),
            pltpu.SemaphoreType.DMA((count, CORES)),
        ],
        cost_estimate=pl.CostEstimate(
            flops=4 * total * width * units,
            bytes_accessed=4 * width * units + 2 * total * width,
            transcendentals=0,
        ),
        compiler_params=pltpu.CompilerParams(vmem_limit_bytes=16 << 20),
        name="second",
    )(hidden, *seconds)


def finish_kernel(chunks, *refs):
    tokens, meta, gain = refs[:3]
    returned, sources = refs[3 : 3 + chunks], refs[3 + chunks : -3]
    out, mixed, query = refs[-3:]
    half = sources[0].shape[0] // 2
    keys = [ref.at[:half] for ref in sources[:6]] + list(sources[6:8])
    values = [ref.at[half:] for ref in sources[:6]] + list(sources[8:10])
    step = pl.program_id(0)
    groups, tok_rows, tile = mixed.shape
    score_scale = HEAD_DIM ** (-0.5)

    @pl.when(step == 0)
    def _():
        placings = [
            (
                meta[n + 1 : n + 2].astype(jnp.int32)
                == lax.broadcasted_iota(jnp.int32, (rows.shape[0], tok_rows), 0)
            ).astype(jnp.bfloat16)
            for n, rows in enumerate(returned)
        ]
        diagonal = lax.broadcasted_iota(
            jnp.int32, (tok_rows, tok_rows), 0
        ) == lax.broadcasted_iota(jnp.int32, (tok_rows, tok_rows), 1)
        gate = jnp.sum(jnp.where(diagonal, meta[0:1], 0.0), axis=1, keepdims=True)
        square = jnp.zeros((tok_rows, 1), jnp.float32)
        for g in range(groups):
            lanes = slice(g * tile, (g + 1) * tile)
            picked = sum(
                lax.dot_general(
                    placing,
                    rows[:, lanes],
                    (((0,), (0,)), ((), ())),
                    preferred_element_type=jnp.float32,
                )
                for placing, rows in zip(placings, returned)
            )
            value = tokens[:, lanes].astype(jnp.float32) + gate * picked
            value = value.astype(jnp.bfloat16)
            mixed[g] = value
            wide = value.astype(jnp.float32)
            square = square + jnp.sum(wide * wide, axis=1, keepdims=True)
        inv_norm = lax.rsqrt(square * (1.0 / (groups * tile)) + 1e-06)
        for g in range(groups):
            lanes = slice(g * tile, (g + 1) * tile)
            value = (mixed[g].astype(jnp.float32) * inv_norm * gain[:, lanes]).astype(jnp.bfloat16)
            query[g] = value * jnp.bfloat16(score_scale)

    low = lax.broadcasted_iota(jnp.int32, (tok_rows, LANES), 1) < HEAD_DIM
    zero = jnp.zeros((tok_rows, LANES), jnp.bfloat16)
    for pair in range(tile // LANES):
        lanes = slice(pair * LANES, (pair + 1) * LANES)
        q = query[step, :, lanes]
        k = jnp.concatenate([ref[:, lanes] for ref in keys], axis=0)
        v = jnp.concatenate([ref[:, lanes] for ref in values], axis=0)
        heads = []
        for head, masked in enumerate((jnp.where(low, q, zero), jnp.where(low, zero, q))):
            scores = lax.dot_general(
                k, masked, (((1,), (1,)), ((), ())), preferred_element_type=jnp.float32
            )
            raw = jnp.exp(scores - jnp.max(scores, axis=0, keepdims=True))
            weight_sum = jnp.sum(raw, axis=0, keepdims=True)
            both = lax.dot_general(
                v,
                raw.astype(jnp.bfloat16),
                (((0,), (0,)), ((), ())),
                preferred_element_type=jnp.float32,
            )
            both = both * (1.0 / weight_sum)
            heads.append(both[head * HEAD_DIM : (head + 1) * HEAD_DIM])
        context = jnp.concatenate(heads, axis=0).T
        out[:, lanes] = (mixed[step, :, lanes].astype(jnp.float32) + context).astype(jnp.bfloat16)


def finish(tokens, meta, gain, returned, sources):
    tok_rows, width = tokens.shape
    tile = 1024
    groups = width // tile
    source_rows = sum(piece.shape[0] for piece in sources) // 2

    def whole(array):
        return pl.BlockSpec(array.shape, lambda i: (0, 0))

    def part(array):
        return pl.BlockSpec((array.shape[0], tile), lambda i: (0, i))

    fixed = [in_hbm(tokens), in_hbm(meta), in_hbm(gain), *returned]
    return pl.pallas_call(
        functools.partial(finish_kernel, len(returned)),
        grid=(groups,),
        in_specs=[whole(a) for a in fixed] + [part(a) for a in sources],
        out_specs=pl.BlockSpec((tok_rows, tile), lambda i: (0, i)),
        out_shape=jax.ShapeDtypeStruct((tok_rows, width), jnp.bfloat16),
        scratch_shapes=[
            pltpu.VMEM((groups, tok_rows, tile), jnp.bfloat16),
            pltpu.VMEM((groups, tok_rows, tile), jnp.bfloat16),
        ],
        cost_estimate=pl.CostEstimate(
            flops=8 * tok_rows * source_rows * width,
            bytes_accessed=4 * source_rows * width + 8 * tok_rows * width,
            transcendentals=tok_rows * source_rows * width // HEAD_DIM,
        ),
        compiler_params=pltpu.CompilerParams(vmem_limit_bytes=20 << 20),
        name="finish",
    )(*fixed, *sources)


def add(one, other):
    return (one.astype(jnp.float32) + other.astype(jnp.float32)).astype(jnp.bfloat16)


def merge_kernel(sides, *refs):
    parts, out, stage = refs[:-2], refs[-2], refs[-1]
    rows, width = parts[0].shape
    groups = width // LANES
    tile = 512
    for side in range(sides):

        def body(i, carry):
            lanes = pl.ds(pl.multiple_of(i * tile, tile), tile)
            value = sum(
                part[:, lanes].astype(jnp.float32) for part in parts[3 * side : 3 * side + 3]
            )
            for lane in range(tile // LANES):
                first = side * rows * groups + i * (tile // LANES) + lane
                stage[pl.ds(first, rows, stride=groups), :] = value[
                    :, lane * LANES : (lane + 1) * LANES
                ]
            return carry

        lax.fori_loop(0, width // tile, body, 0, unroll=4)
    out[...] = stage[...].astype(jnp.bfloat16).reshape(out.shape)


def merge(parts, experts):
    rows, width = parts[0].shape
    sides = len(parts) // 3
    total = sides * rows * width // LANES
    near = pl.BlockSpec(memory_space=pltpu.VMEM)
    return pl.pallas_call(
        functools.partial(merge_kernel, sides),
        in_specs=[near] * len(parts),
        out_specs=near,
        out_shape=jax.ShapeDtypeStruct((experts, total // experts, LANES), jnp.bfloat16),
        scratch_shapes=[pltpu.VMEM((total, LANES), jnp.float32)],
        cost_estimate=pl.CostEstimate(
            flops=3 * total * LANES, bytes_accessed=8 * total * LANES, transcendentals=0
        ),
        compiler_params=pltpu.CompilerParams(vmem_limit_bytes=8 << 20),
        name="merge",
    )(*parts)


def exchange(blocks):
    return lax.all_to_all(blocks, "expert", split_axis=0, concat_axis=0, tiled=True)


def per_device(tokens, expert_id, gate, w_in, w_out, keys, values, query_gain):
    tok_rows, model_width = tokens.shape
    meta, *outgoing = prepare(expert_id.reshape(1, tok_rows), gate[None, :], tokens)

    firsts, seconds = [
        [in_hbm(w) for w in (own, swap_cores(own))]
        for own in (w_in[0], w_out[0])
    ]

    pairs = jnp.concatenate([keys, values])
    half = keys.shape[0]
    near = shift(pairs, 1)
    back = shift(pairs, -1)
    far_keys = shift(near[:half], 1)
    far_values = shift(back[half:], -1)
    sources = []
    for piece in (pairs, near, back, far_keys, far_values):
        sources.extend((piece, swap_cores(piece)))

    returned = []
    arrived = [exchange(blocks) for blocks in outgoing]

    def whole_blocks(blocks):
        own = blocks.reshape(-1, model_width)
        half = own.shape[0] // 2
        near = shift(own, 1)
        back = shift(own, -1)
        low = shift(near[:half], 1)
        high = shift(back[half:], -1)
        parts = (own, near, back, low, high)
        hidden = first_layer(parts, firsts)
        parts = second_layer(hidden, seconds, [part.shape[0] for part in parts])
        own, near, back, low, high = parts
        low = shift(low, -1)
        high = shift(high, 1)
        near = shift(jnp.concatenate([add(near[:half], low), near[half:]]), -1)
        back = shift(jnp.concatenate([back[:half], add(back[half:], high)]), 1)
        summed = merge((own, near, back), blocks.shape[0])
        return exchange(summed).reshape(-1, model_width)

    for n, blocks in enumerate(arrived):
        experts = blocks.shape[0]
        if n > 0:
            returned.append(whole_blocks(blocks))
            continue
        a, b = [
            half.reshape(-1, model_width)
            for half in (blocks[: experts // 2], blocks[experts // 2 :])
        ]
        near_a = shift(a, 1)
        back_b = shift(b, -1)
        near_b = shift(b, 1)
        back_a = shift(a, -1)
        low = shift(near_a, 1)
        high = shift(back_b, -1)
        halves = (a, b, near_a, near_b, back_a, back_b, low, high)
        hidden = first_layer(halves, firsts)
        halves = second_layer(hidden, seconds, [half.shape[0] for half in halves])
        a, b, near_a, near_b, back_a, back_b, low, high = halves
        low = shift(low, -1)
        high = shift(high, 1)
        near_b = shift(near_b, -1)
        back_a = shift(back_a, 1)
        near_a = shift(add(near_a, low), -1)
        back_b = shift(add(back_b, high), 1)
        summed = merge((a, near_a, back_a, b, near_b, back_b), experts)
        answers = exchange(summed)
        returned.append(answers.reshape(-1, model_width))

    return finish(
        tokens,
        meta,
        query_gain[None, :],
        returned,
        sources,
    )


def solution(mesh):
    return jax.shard_map(
        per_device,
        mesh=mesh,
        in_specs=(
            P(("expert", "src"), None),
            P(("expert", "src"), None),
            P(("expert", "src")),
            P("expert", None, "src"),
            P("expert", "src", None),
            P(("expert", "src"), None),
            P(("expert", "src"), None),
            P(),
        ),
        out_specs=P(("expert", "src"), None),
        check_vma=False,
    )
```
